32 devices in a mesh: gx: 2 (over x), gy: 2 (over core), gz: 8 (over z, y).
Axes of the slice: x: 2, y: 2, z: 4, core: 2. Of those that a mesh axis runs over, the one named last changes fastest.
Arguments:
- state: float32 [24, 32, 16, 512], P(None, 'gx', ('gy', 'gz')), may hold values from -6 to 6
- base: float32 [24, 32, 16, 512], P(None, 'gx', ('gy', 'gz')), may hold values from -0.6 to 0.6
- accum: float32 [24, 32, 16, 512], P(None, 'gx', ('gy', 'gz')), may hold values from -0.3 to 0.3
- owner: int32 [8], replicated, may hold values from 0 to 7, each once
Outputs:
- next_section: float32 [24, 32, 16, 512], P(None, 'gx', ('gy', 'gz'))
- accum_out: float32 [24, 32, 16, 512], P(None, 'gx', ('gy', 'gz'))
The draws below stay inside these ranges and needn't reach their ends.
Inputs may be any that keep to these rules, and one draw needn't show every extreme that they name: owner names every index of gz once.
All inputs are finite; a program needn't handle non-finite values.
Results may differ from the reference program's by a relative error of at most 0.00002.
Values sent between devices are 32-bit elements; how exact they have to be, the bound alone decides.
No kernel may reach another device: no remote copies, remote signals or barrier semaphores. Data moves between devices by JAX's collectives and lax.ppermute only.
A program may use at most 192 MiB of HBM per device.

```python
import jax
import jax.numpy as jnp
from jax import lax

FIELDS = 24
BLOCK = 16
NX = 32
TILES = 16
TILE_CELLS = 512
N_GY = 2
N_GZ = 8


def block_scale(rng, shape, pieces, smallest, top_value):
    level, own = 1.0, jax.random.fold_in(rng, 6)
    for dim, blocks in pieces:
        draws = jnp.exp(jax.random.uniform(jax.random.fold_in(own, dim), (blocks,), jnp.float32, smallest / len(pieces), top_value / len(pieces)))
        level = level * jnp.repeat(draws, shape[dim] // blocks).reshape([-1 if axis == dim else 1 for axis in range(len(shape))])
    return level


def centred(own_key, shape, spread, bound, cuts=(), dtype=jnp.bfloat16):
    values = spread * jax.random.normal(own_key, shape, jnp.float32)
    if cuts:
        values = values * block_scale(own_key, shape, cuts, -0.22, 0.18)
    return jnp.clip(values, -bound, bound).astype(dtype)


def setup_inputs(seed: int = 0) -> dict:
    arg_keys = jax.random.split(jax.random.key(seed), 5)
    return {
        "state": centred(arg_keys[0], (FIELDS, NX, TILES, TILE_CELLS), 1.0, 6.0, ((1, 2), (2, 16)), jnp.float32),
        "base": centred(arg_keys[1], (FIELDS, NX, TILES, TILE_CELLS), 0.1, 0.6, ((1, 2), (2, 16)), jnp.float32),
        "accum": centred(arg_keys[2], (FIELDS, NX, TILES, TILE_CELLS), 0.05, 0.3, ((1, 2), (2, 16)), jnp.float32),
        "owner": jax.random.permutation(arg_keys[3], N_GZ).astype(jnp.int32),
    }


DAMPING_STRENGTH = 1.0
SPACING = 1.0
TIME_STEP = 0.25
SECTION_SHIFT = 0.5
SECTION_WEIGHT = 1.0 / 3.0


def shifted(padded, dimension, offset):
    selection = [slice(None)]
    for axis_index in range(1, 4):
        length = padded.shape[axis_index] - 6
        start_at = 3 + (offset if axis_index == dimension else 0)
        selection.append(slice(start_at, start_at + length))
    return padded[tuple(selection)]


def stencils(padded):
    laplace = 0.0
    damping = 0.0
    for dimension in (1, 2, 3):
        values = [shifted(padded, dimension, offset) for offset in range(-3, 4)]
        laplace = laplace + (-values[1] + 16.0 * values[2] - 30.0 * values[3] + 16.0 * values[4] - values[5]) / (12.0 * SPACING * SPACING)
        damping = damping + (values[0] - 6.0 * values[1] + 15.0 * values[2] - 20.0 * values[3] + 15.0 * values[4] - 6.0 * values[5] + values[6]) * (DAMPING_STRENGTH / (64.0 * SPACING))
    return laplace, damping


def rates_from(centre, laplace, damping):
    halves = centre.shape[0] // 2
    metric = centre[:halves]
    curvature = centre[halves:]
    lapse_value = 1.0 + 0.25 * jnp.tanh(metric[0])
    trace_value = jnp.mean(curvature, axis=0)
    metric_rate = -2.0 * lapse_value * curvature + damping[:halves]
    curvature_rate = -0.5 * lapse_value * laplace[:halves] + lapse_value * trace_value * curvature + damping[halves:]
    return jnp.concatenate([metric_rate, curvature_rate], axis=0)


def to_grid(stored, owner):
    fields = stored.shape[0]
    cells_x = stored.shape[1]
    side_y = BLOCK
    side_z = 2 * BLOCK
    blocked = stored.reshape(fields, cells_x, N_GY, N_GZ, side_y, side_z)
    ordered = jnp.take(blocked, owner, axis=3)
    whole_grid = ordered.transpose(0, 1, 2, 4, 3, 5)
    return whole_grid.reshape(fields, cells_x, N_GY * side_y, N_GZ * side_z)


def from_grid(whole_grid, owner):
    fields = whole_grid.shape[0]
    cells_x = whole_grid.shape[1]
    side_y = BLOCK
    side_z = 2 * BLOCK
    tiled = whole_grid.reshape(fields, cells_x, N_GY, side_y, N_GZ, side_z)
    tiled = tiled.transpose(0, 1, 2, 4, 3, 5)
    stored = jnp.zeros_like(tiled).at[:, :, :, owner].set(tiled)
    return stored.reshape(fields, cells_x, N_GY * N_GZ, side_y * side_z)


def per_field(single):
    laplace, damping = stencils(single[None])
    return laplace[0], damping[0]


def reference(state, base, accum, owner):
    whole_grid = to_grid(state, owner)
    padded = jnp.pad(whole_grid, ((0, 0), (3, 3), (3, 3), (3, 3)), mode="wrap")
    laplace, damping = lax.map(per_field, padded)
    rate_values = rates_from(whole_grid, laplace, damping)
    stored = from_grid(rate_values, owner)
    next_section = base + (SECTION_SHIFT * TIME_STEP) * stored
    accum_out = accum + (SECTION_WEIGHT * TIME_STEP) * stored
    return next_section, accum_out
```

```python
import functools

import jax
import jax.numpy as jnp
from jax import lax
from jax.experimental import pallas as pl
from jax.experimental.pallas import tpu as pltpu
from jax.sharding import PartitionSpec as P

BLOCK = 16


DAMPING_STRENGTH = 1.0
SPACING = 1.0
TIME_STEP = 0.25
SECTION_SHIFT = 0.5
SECTION_WEIGHT = 1.0 / 3.0

LANES = 128
GHOST = 3
SLOT = 2 * GHOST
DEPTH = 2 * BLOCK
SLOTS = DEPTH // SLOT
DAMP = DAMPING_STRENGTH / (64.0 * SPACING)
LAPL = 1.0 / (12.0 * SPACING * SPACING)
VMEM = pltpu.VMEM
SMEM = pltpu.SMEM


def vmem_spec():
    return pl.BlockSpec(memory_space=VMEM)


def call(kernel, name, outs, in_specs, out_specs=None, scratch=(), cost=None, aliases=None):
    multiple = isinstance(outs, (list, tuple))
    if out_specs is None:
        out_specs = [vmem_spec() for _ in outs] if multiple else vmem_spec()
    return pl.pallas_call(
        kernel,
        name=name,
        out_shape=outs,
        in_specs=in_specs,
        out_specs=out_specs,
        scratch_shapes=list(scratch),
        input_output_aliases=aliases or {},
        cost_estimate=pl.CostEstimate(flops=cost[0], bytes_accessed=cost[1], transcendentals=0),
    )


def lane_index(rows):
    return lax.broadcasted_iota(jnp.int32, (rows, LANES), 1)


def pack_faces_kernel(state_ref, out_ref):
    fields, rows, _ = state_ref.shape
    slot = (lane_index(rows) % DEPTH) // SLOT
    for group in range(out_ref.shape[0]):
        packed = jnp.zeros((rows, LANES), jnp.float32)
        for j in range(min(SLOTS, fields - group * SLOTS)):
            moved = pltpu.roll(state_ref[group * SLOTS + j], GHOST + SLOT * j, 1)
            packed = jnp.where(slot == j, moved, packed)
        out_ref[group] = packed


def pack_ends_kernel(per_layer, state_ref, layers_ref, strips_ref):
    fields, rows, _ = state_ref.shape
    edge = GHOST * per_layer
    layers = rows // per_layer
    layers_ref[:, :edge] = state_ref[:, :edge]
    layers_ref[:, edge:] = state_ref[:, rows - edge :]
    for f in range(fields):
        strips_ref[f, :layers] = state_ref[f, pl.ds(0, layers, stride=per_layer)]
        strips_ref[f, layers:] = state_ref[f, pl.ds(per_layer - 1, layers, stride=per_layer)]


def find_column(owner_ref, device, columns):
    def body(t, found):
        return jnp.where(owner_ref[t] == device, t, found)

    return lax.fori_loop(0, columns, body, jnp.int32(0))


def neighbours(owner_ref, device, columns):
    column = find_column(owner_ref, device, columns)
    below = owner_ref[lax.rem(column + columns - 1, columns)]
    above = owner_ref[lax.rem(column + 1, columns)]
    return below, above


def forward_kernel(columns, cross, owner_ref, me_ref, *refs):
    *sources, out_ref = refs
    me = me_ref[0]
    below, above = neighbours(owner_ref, me ^ cross, columns)
    rows = out_ref.shape[1]
    low_part = (lane_index(rows) % DEPTH) % SLOT < GHOST
    low_from = me ^ below
    high_from = me ^ above
    out_ref[...] = sources[0][...]
    for d, source in enumerate(sources):

        @pl.when(low_from == d)
        def _():
            for g in range(out_ref.shape[0]):
                out_ref[g] = jnp.where(low_part, source[g], out_ref[g])

        @pl.when(high_from == d)
        def _():
            for g in range(out_ref.shape[0]):
                out_ref[g] = jnp.where(low_part, out_ref[g], source[g])


def center_kernel(
    per_layer, state_ref, layers_ref, strips_ref, base_ref, accum_ref, next_ref, total_ref, half_ref,
    wide_ref, after_ref, before_ref,
):
    fields, rows, _ = state_ref.shape
    halves = fields // 2
    edge = GHOST * per_layer
    layers = rows // per_layer
    lane = lane_index(rows)
    depth = lane % DEPTH
    lapse = 1.0 + 0.25 * jnp.tanh(state_ref[0])
    trace = state_ref[halves]
    for f in range(halves + 1, fields):
        trace = trace + state_ref[f]
    pull = lapse * trace * (1.0 / halves)
    half_ref[...] = -0.5 * lapse

    def stencil_sums(f):
        here = state_ref[f]
        wide_ref[edge : edge + rows] = here
        wide_ref[:edge] = layers_ref[f, edge:]
        wide_ref[edge + rows :] = layers_ref[f, :edge]
        after_ref[...] = wide_ref[edge + 1 : edge + 1 + rows]
        before_ref[...] = wide_ref[edge - 1 : edge - 1 + rows]
        after_ref[pl.ds(per_layer - 1, layers, stride=per_layer)] = strips_ref[f, :layers]
        before_ref[pl.ds(0, layers, stride=per_layer)] = strips_ref[f, layers:]
        after = after_ref[...]
        before = before_ref[...]
        sums = []
        for k in range(1, GHOST + 1):
            low = edge - k * per_layer
            high = edge + k * per_layer
            total = wide_ref[low : low + rows] + wide_ref[high : high + rows]
            step = DEPTH * k
            total += pltpu.roll(jnp.where(lane >= step, here, after), LANES - step, 1)
            total += pltpu.roll(jnp.where(lane < LANES - step, here, before), step, 1)
            total += pltpu.roll(jnp.where(depth >= k, here, 0.0), LANES - k, 1)
            total += pltpu.roll(jnp.where(depth < DEPTH - k, here, 0.0), k, 1)
            sums.append(total)
        return here, sums

    def write(f, rate):
        next_ref[f] = base_ref[f] + (SECTION_SHIFT * TIME_STEP) * rate
        total_ref[f] = accum_ref[f] + (SECTION_WEIGHT * TIME_STEP) * rate

    def body(f, carry):
        u, sums = stencil_sums(f)
        damping = (sums[2] - 6.0 * sums[1] + 15.0 * sums[0] - 60.0 * u) * DAMP
        laplace = (16.0 * sums[0] - sums[1] - 90.0 * u) * LAPL
        v = state_ref[f + halves]
        write(f, -2.0 * lapse * v + damping)
        v, sums = stencil_sums(f + halves)
        damping = (sums[2] - 6.0 * sums[1] + 15.0 * sums[0] - 60.0 * v) * DAMP
        write(f + halves, -0.5 * lapse * laplace + pull * v + damping)
        return carry

    lax.fori_loop(0, halves, body, 0)


def select_source(index, sources, dest_ref):
    for d, source in enumerate(sources):

        @pl.when(index == d)
        def _():
            dest_ref[...] = source[...]


def final_kernel(
    columns, owner_ref, me_ref, half_ref, next_ref, total_ref, *refs
):
    count = len(refs) - 9
    sources = refs[:count]
    next_out, total_out, low_ref, high_ref, damp_ref, lapl_ref, next_buf, total_buf, sems = refs[count:]
    fields, rows, _ = next_ref.shape
    halves = fields // 2
    groups = low_ref.shape[0]
    me = me_ref[0]
    below, above = neighbours(owner_ref, me, columns)
    low_from = me ^ below
    high_from = me ^ above
    select_source(jnp.where(low_from < count, low_from, 0), sources, low_ref)
    select_source(jnp.where(high_from < count, high_from, 0), sources, high_ref)
    lane = lane_index(rows)
    depth = lane % DEPTH
    slot = (depth + DEPTH - SLOT) % DEPTH
    low_at = jnp.where(slot < SLOTS * SLOT, slot % SLOT, SLOT)
    high_at = jnp.where(depth < SLOTS * SLOT, depth % SLOT, 0)

    def per_lane(position, values):
        out = jnp.zeros((rows, LANES), jnp.float32)
        for at, value in values:
            out = jnp.where(position == at, value, out)
        return out

    low_damp = [
        per_lane(low_at, v)
        for v in (
            ((0, 1.0 * DAMP), (1, 1.0 * DAMP), (2, 1.0 * DAMP)),
            ((0, -6.0 * DAMP), (1, -6.0 * DAMP)),
            ((0, 15.0 * DAMP),),
        )
    ]
    high_damp = [
        per_lane(high_at, v)
        for v in (
            ((3, 1.0 * DAMP), (4, 1.0 * DAMP), (5, 1.0 * DAMP)),
            ((4, -6.0 * DAMP), (5, -6.0 * DAMP)),
            ((5, 15.0 * DAMP),),
        )
    ]
    low_lapl = [per_lane(low_at, v) for v in (((0, -LAPL), (1, -LAPL)), ((0, 16.0 * LAPL),))]
    high_lapl = [per_lane(high_at, v) for v in (((4, -LAPL), (5, -LAPL)), ((5, 16.0 * LAPL),))]
    shift = 2 * DEPTH + SLOT
    for g in range(groups):
        low = low_ref[g]
        high = high_ref[g]
        low_0 = pltpu.roll(low, shift, 1)
        low_1 = pltpu.roll(low, shift - 1, 1)
        low_2 = pltpu.roll(low, shift - 2, 1)
        high_1 = pltpu.roll(high, 1, 1)
        high_2 = pltpu.roll(high, 2, 1)
        damp_ref[g] = (
            low_damp[0] * low_0 + low_damp[1] * low_1 + low_damp[2] * low_2
            + high_damp[0] * high + high_damp[1] * high_1 + high_damp[2] * high_2
        )
        if g * SLOTS < halves:
            lapl_ref[g] = (
                low_lapl[0] * low_1 + low_lapl[1] * low_2
                + high_lapl[0] * high_1 + high_lapl[1] * high_2
            )
    at_edge = (depth < GHOST) | (depth >= DEPTH - GHOST)
    half = half_ref[...]

    def spread(ref, f):
        moved = pltpu.roll(ref[f // SLOTS], (DEPTH - SLOT - SLOT * (f % SLOTS)) % LANES, 1)
        return jnp.where(at_edge, moved, 0.0)

    copies = []
    chunk = halves // 2
    for start in range(0, fields, chunk):
        for f in range(start, start + chunk):
            rate = spread(damp_ref, f)
            if f >= halves:
                rate = rate + half * spread(lapl_ref, f - halves)
            next_buf[f] = next_ref[f] + (SECTION_SHIFT * TIME_STEP) * rate
            total_buf[f] = total_ref[f] + (SECTION_WEIGHT * TIME_STEP) * rate
        part = pl.ds(start, chunk)
        for which, (buf, out) in enumerate(((next_buf, next_out), (total_buf, total_out))):
            copy = pltpu.make_async_copy(buf.at[part], out.at[part], sems.at[which, start // chunk])
            copy.start()
            copies.append(copy)
    for copy in copies:
        copy.wait()


def swap_ends(ends, axis):
    count = lax.axis_size(axis)
    if count == 2:
        return lax.ppermute(ends, axis, [(0, 1), (1, 0)])
    low, high = jnp.split(ends, 2, axis=1)
    forward = [(i, (i + 1) % count) for i in range(count)]
    backward = [(target, source) for source, target in forward]
    return jnp.concatenate([lax.ppermute(low, axis, backward), lax.ppermute(high, axis, forward)], axis=1)


def routed(packed, owner):
    columns = lax.axis_size("gz")
    labels = jnp.arange(columns, dtype=jnp.int32)
    matches = owner[:, None] == labels[None, :]
    column_of = jnp.sum(jnp.where(matches, labels[:, None], 0), axis=0)
    below = jnp.take(owner, (column_of + columns - 1) % columns)
    above = jnp.take(owner, (column_of + 1) % columns)
    groups, rows, _ = packed.shape
    pieces = packed.reshape(groups, columns, rows // columns, LANES).transpose(1, 0, 2, 3)
    spread = lax.all_to_all(pieces, "gz", split_axis=0, concat_axis=0, tiled=True)
    low_part = (jnp.arange(LANES) % DEPTH) % SLOT < GHOST
    forwarded = jnp.where(low_part, spread[below], spread[above])
    arrived = lax.all_to_all(forwarded, "gz", split_axis=0, concat_axis=0, tiled=True)
    return arrived.transpose(1, 0, 2, 3).reshape(groups, rows, LANES)


def local(state, base, accum, owner):
    fields, thickness, _, cells = state.shape
    per_layer = cells // LANES
    rows = thickness * per_layer
    shape = (fields, rows, LANES)
    columns = lax.axis_size("gz")
    me = lax.axis_index("gz").reshape(1).astype(jnp.int32)
    cells_in = state.reshape(shape)
    groups = -(-fields // SLOTS)
    f32 = lambda *s: jax.ShapeDtypeStruct(s, jnp.float32)
    whole = fields * rows * LANES * 4
    smem = pl.BlockSpec(memory_space=SMEM)
    anywhere = pl.BlockSpec(memory_space=pl.ANY)

    packed = call(
        pack_faces_kernel, "pack_faces", f32(groups, rows, LANES), [vmem_spec()], cost=(whole, whole)
    )(cells_in)
    if columns <= 8 and columns & (columns - 1) == 0 and columns > 2:
        near = columns // 2
        cross = columns // 2 + columns // 4
        exchange = lambda x, d: lax.ppermute(x, "gz", [(i, i ^ d) for i in range(columns)])
        got = {d: exchange(packed, d) for d in sorted(range(1, near), reverse=True)}
        sources = [packed] + [got[d] for d in range(1, near)]
        forwarded = call(
            functools.partial(forward_kernel, columns, cross), "forward", f32(groups, rows, LANES),
            [smem, smem] + [vmem_spec() for _ in sources], cost=(whole, whole),
        )(owner, me, *sources)
        candidates = [exchange(forwarded, cross)] + sources[1:]
    else:
        candidates = [routed(packed, owner)]

    cells_in, packed = lax.optimization_barrier((cells_in, packed))
    layers, strips = call(
        functools.partial(pack_ends_kernel, per_layer), "pack_ends",
        [f32(fields, 2 * GHOST * per_layer, LANES), f32(fields, 2 * thickness, LANES)],
        [vmem_spec()], cost=(whole, whole),
    )(cells_in)
    layers = swap_ends(layers, "gx")
    strips = swap_ends(strips, "gy")
    part_next, part_total, half = call(
        functools.partial(center_kernel, per_layer), "center",
        [f32(*shape), f32(*shape), f32(rows, LANES)],
        [vmem_spec() for _ in range(5)],
        scratch=[VMEM((rows + 2 * GHOST * per_layer, LANES), jnp.float32), VMEM((rows, LANES), jnp.float32), VMEM((rows, LANES), jnp.float32)],
        cost=(60 * whole, 6 * whole),
    )(cells_in, layers, strips, base.reshape(shape), accum.reshape(shape))
    next_section, accum_out = call(
        functools.partial(final_kernel, columns), "final", [f32(*shape), f32(*shape)],
        [smem, smem] + [vmem_spec() for _ in range(3 + len(candidates))],
        out_specs=[anywhere, anywhere],
        scratch=[VMEM((groups, rows, LANES), jnp.float32) for _ in range(3)]
        + [VMEM((-(-(fields // 2) // SLOTS), rows, LANES), jnp.float32)]
        + [VMEM(shape, jnp.float32) for _ in range(2)]
        + [pltpu.SemaphoreType.DMA((2, 4))],
        cost=(10 * whole, 4 * whole),
    )(owner, me, half, part_next, part_total, *candidates)
    return (next_section.reshape(state.shape), accum_out.reshape(state.shape))


def solution(mesh):
    return jax.shard_map(
        local,
        mesh=mesh,
        in_specs=(
            P(None, "gx", ("gy", "gz"), None),
            P(None, "gx", ("gy", "gz"), None),
            P(None, "gx", ("gy", "gz"), None),
            P(),
        ),
        out_specs=(P(None, "gx", ("gy", "gz"), None), P(None, "gx", ("gy", "gz"), None)),
        check_vma=False,
    )
```

```python
import functools

import jax
import jax.numpy as jnp
from jax import lax
from jax.experimental import pallas as pl
from jax.experimental.pallas import tpu as pltpu
from jax.sharding import PartitionSpec as P


BLOCK = 16


DAMPING_STRENGTH = 1.0
SPACING = 1.0
TIME_STEP = 0.25
SECTION_SHIFT = 0.5
SECTION_WEIGHT = 1.0 / 3.0

LANES = 128
GHOST = 3
SLOT = 2 * GHOST
DEPTH = 2 * BLOCK
SLOTS = DEPTH // SLOT
DAMP = DAMPING_STRENGTH / (64.0 * SPACING)
LAPL = 1.0 / (12.0 * SPACING * SPACING)
VMEM = pltpu.VMEM
SMEM = pltpu.SMEM


def vmem_spec():
    return pl.BlockSpec(memory_space=VMEM)


def call(kernel, outs, in_specs, out_specs=None, scratch=(), cost=None, aliases=None):
    multiple = isinstance(outs, (list, tuple))
    if out_specs is None:
        out_specs = [vmem_spec() for _ in outs] if multiple else vmem_spec()
    return pl.pallas_call(
        kernel,
        out_shape=outs,
        in_specs=in_specs,
        out_specs=out_specs,
        scratch_shapes=list(scratch),
        input_output_aliases=aliases or {},
        compiler_params=pltpu.CompilerParams(vmem_limit_bytes=16 * 1024 * 1024),
        cost_estimate=pl.CostEstimate(flops=cost[0], bytes_accessed=cost[1], transcendentals=0),
    )


def lane_index(rows):
    return lax.broadcasted_iota(jnp.int32, (rows, LANES), 1)


def pack_faces_kernel(state_ref, out_ref):
    fields, rows, _ = state_ref.shape
    slot = (lane_index(rows) % DEPTH) // SLOT
    for group in range(out_ref.shape[0]):
        packed = jnp.zeros((rows, LANES), jnp.float32)
        for j in range(min(SLOTS, fields - group * SLOTS)):
            moved = pltpu.roll(state_ref[group * SLOTS + j], GHOST + SLOT * j, 1)
            packed = jnp.where(slot == j, moved, packed)
        out_ref[group] = packed


def pack_ends_kernel(per_layer, state_ref, layers_ref, strips_ref):
    fields, rows, _ = state_ref.shape
    edge = GHOST * per_layer
    layers = rows // per_layer
    layers_ref[:, :edge] = state_ref[:, :edge]
    layers_ref[:, edge:] = state_ref[:, rows - edge :]
    for f in range(fields):
        strips_ref[f, :layers] = state_ref[f, pl.ds(0, layers, stride=per_layer)]
        strips_ref[f, layers:] = state_ref[f, pl.ds(per_layer - 1, layers, stride=per_layer)]


def find_column(owner_ref, device, columns):
    def body(t, found):
        return jnp.where(owner_ref[t] == device, t, found)

    return lax.fori_loop(0, columns, body, jnp.int32(0))


def neighbours(owner_ref, device, columns):
    column = find_column(owner_ref, device, columns)
    below = owner_ref[lax.rem(column + columns - 1, columns)]
    above = owner_ref[lax.rem(column + 1, columns)]
    return below, above


def source_masks(lanes, low_from, high_from, count):
    chosen = jnp.where(lanes, low_from, high_from)
    return [chosen == d for d in range(1, count)]


def forward_kernel(columns, cross, owner_ref, me_ref, *refs):
    *sources, out_ref = refs
    me = me_ref[0]
    below, above = neighbours(owner_ref, me ^ cross, columns)
    low_part = (lane_index(out_ref.shape[1]) % DEPTH) % SLOT < GHOST
    masks = source_masks(low_part, me ^ below, me ^ above, len(sources))
    for g in range(out_ref.shape[0]):
        chosen = sources[0][g]
        for mask, source in zip(masks, sources[1:]):
            chosen = jnp.where(mask, source[g], chosen)
        out_ref[g] = chosen


def field_sums(per_layer, lane, state_ref, strips_ref, f, wide_ref, after_ref, before_ref):
    rows = state_ref.shape[1]
    edge = GHOST * per_layer
    layers = rows // per_layer
    depth = lane % DEPTH
    here = state_ref[f]
    wide_ref[edge : edge + rows] = here
    after_ref[...] = wide_ref[edge + 1 : edge + 1 + rows]
    before_ref[...] = wide_ref[edge - 1 : edge - 1 + rows]
    after_ref[pl.ds(per_layer - 1, layers, stride=per_layer)] = strips_ref[f, :layers]
    before_ref[pl.ds(0, layers, stride=per_layer)] = strips_ref[f, layers:]
    after = after_ref[...]
    before = before_ref[...]
    sums = []
    for k in range(1, GHOST + 1):
        low = edge - k * per_layer
        high = edge + k * per_layer
        total = wide_ref[low : low + rows] + wide_ref[high : high + rows]
        step = DEPTH * k
        total += pltpu.roll(jnp.where(lane >= step, here, after), LANES - step, 1)
        total += pltpu.roll(jnp.where(lane < LANES - step, here, before), step, 1)
        total += pltpu.roll(jnp.where(depth >= k, here, 0.0), LANES - k, 1)
        total += pltpu.roll(jnp.where(depth < DEPTH - k, here, 0.0), k, 1)
        sums.append(total)
    return here, sums


def pair_rates(here, curvature, metric_sums, curvature_sums, half, pull):
    one, two, three = metric_sums
    damping = (three - 6.0 * two + 15.0 * one - 60.0 * here) * DAMP
    laplace = (16.0 * one - two - 90.0 * here) * LAPL
    metric_rate = 4.0 * half * curvature + damping
    one, two, three = curvature_sums
    damping = (three - 6.0 * two + 15.0 * one - 60.0 * curvature) * DAMP
    return metric_rate, half * laplace + pull * curvature + damping


def early_kernel(
    per_layer, count, state_ref, strips_ref, base_ref, accum_ref, next_ref, total_ref, half_ref, pull_ref,
    wide_ref, after_ref, before_ref,
):
    fields, rows, _ = state_ref.shape
    halves = fields // 2
    edge = GHOST * per_layer
    lane = lane_index(rows)
    lapse = 1.0 + 0.25 * jnp.tanh(state_ref[0])
    trace = state_ref[halves]
    for f in range(halves + 1, fields):
        trace = trace + state_ref[f]
    half_ref[...] = -0.5 * lapse
    pull_ref[...] = lapse * trace * (1.0 / halves)
    wide_ref[:edge] = jnp.zeros((edge, LANES), jnp.float32)
    wide_ref[edge + rows :] = jnp.zeros((edge, LANES), jnp.float32)

    def body(f, carry):
        sums = lambda at: field_sums(per_layer, lane, state_ref, strips_ref, at, wide_ref, after_ref, before_ref)
        u, u_sums = sums(f)
        v, v_sums = sums(f + halves)
        rates = pair_rates(u, v, u_sums, v_sums, half_ref[...], pull_ref[...])
        for at, rate in zip((f, f + halves), rates):
            next_ref[at] = base_ref[at] + (SECTION_SHIFT * TIME_STEP) * rate
            total_ref[at] = accum_ref[at] + (SECTION_WEIGHT * TIME_STEP) * rate
        return carry

    lax.fori_loop(0, count, body, 0)


def late_kernel(
    per_layer, count, state_ref, layers_ref, strips_ref, base_ref, accum_ref, half_ref, pull_ref, next_in, total_in,
    next_ref, total_ref, wide_ref, after_ref, before_ref, low_ref, high_ref,
):
    fields, rows, _ = state_ref.shape
    halves = fields // 2
    edge = GHOST * per_layer
    reach = -(-edge // 8) * 8
    lane = lane_index(rows)
    low_ref[edge:] = jnp.zeros((reach, LANES), jnp.float32)
    high_ref[:reach] = jnp.zeros((reach, LANES), jnp.float32)

    def ends(f):
        low_ref[:edge] = layers_ref[f, edge:]
        high_ref[reach:] = layers_ref[f, :edge]
        out = []
        for buf, at in ((low_ref, lambda k: edge - k * per_layer), (high_ref, lambda k: k * per_layer)):
            one, two, three = (buf[at(k) : at(k) + reach] for k in (1, 2, 3))
            out.append(((three - 6.0 * two + 15.0 * one) * DAMP, (16.0 * one - two) * LAPL))
        return out

    def mend(f, carry):
        for at, u, v in zip((slice(0, reach), slice(rows - reach, rows)), ends(f), ends(f + halves)):
            for field, rate in ((f, u[0]), (f + halves, v[0] + half_ref[at] * u[1])):
                next_ref[field, at] = next_in[field, at] + (SECTION_SHIFT * TIME_STEP) * rate
                total_ref[field, at] = total_in[field, at] + (SECTION_WEIGHT * TIME_STEP) * rate
        return carry

    lax.fori_loop(0, count, mend, 0)

    def body(f, carry):
        def sums(at):
            wide_ref[:edge] = layers_ref[at, edge:]
            wide_ref[edge + rows :] = layers_ref[at, :edge]
            return field_sums(per_layer, lane, state_ref, strips_ref, at, wide_ref, after_ref, before_ref)

        u, u_sums = sums(f)
        v, v_sums = sums(f + halves)
        rates = pair_rates(u, v, u_sums, v_sums, half_ref[...], pull_ref[...])
        for at, rate in zip((f, f + halves), rates):
            next_ref[at] = base_ref[at] + (SECTION_SHIFT * TIME_STEP) * rate
            total_ref[at] = accum_ref[at] + (SECTION_WEIGHT * TIME_STEP) * rate
        return carry

    lax.fori_loop(count, halves, body, 0)


def final_kernel(columns, owner_ref, me_ref, half_ref, next_ref, total_ref, *refs):
    count = len(refs) - 6
    sources = refs[:count]
    next_out, total_out, lapl_ref, next_buf, total_buf, sems = refs[count:]
    fields, rows, _ = next_ref.shape
    halves = fields // 2
    groups = sources[0].shape[0]
    me = me_ref[0]
    below, above = neighbours(owner_ref, me, columns)
    low_from = me ^ below
    high_from = me ^ above
    one_lane = lane_index(8)
    depth = one_lane % DEPTH
    slot = (depth + DEPTH - SLOT) % DEPTH
    low_at = jnp.where(slot < SLOTS * SLOT, slot % SLOT, SLOT)
    high_at = jnp.where(depth < SLOTS * SLOT, depth % SLOT, 0)

    def widen(x):
        return jnp.concatenate([x] * (rows // 8), axis=0)

    def per_lane(position, values):
        out = jnp.zeros((8, LANES), jnp.float32)
        for at, value in values:
            out = jnp.where(position == at, value, out)
        return widen(out)

    low_damp = [
        per_lane(low_at, v)
        for v in (
            ((0, 1.0 * DAMP), (1, 1.0 * DAMP), (2, 1.0 * DAMP)),
            ((0, -6.0 * DAMP), (1, -6.0 * DAMP)),
            ((0, 15.0 * DAMP),),
        )
    ]
    high_damp = [
        per_lane(high_at, v)
        for v in (
            ((3, 1.0 * DAMP), (4, 1.0 * DAMP), (5, 1.0 * DAMP)),
            ((4, -6.0 * DAMP), (5, -6.0 * DAMP)),
            ((5, 15.0 * DAMP),),
        )
    ]
    low_lapl = [per_lane(low_at, v) for v in (((0, -LAPL), (1, -LAPL)), ((0, 16.0 * LAPL),))]
    high_lapl = [per_lane(high_at, v) for v in (((4, -LAPL), (5, -LAPL)), ((5, 16.0 * LAPL),))]
    low_masks = [jnp.full((rows, LANES), low_from) == d for d in range(1, count)]
    high_masks = [jnp.full((rows, LANES), high_from) == d for d in range(1, count)]
    at_edge = widen(((depth < GHOST) | (depth >= DEPTH - GHOST)).astype(jnp.float32)) > 0.5
    half = half_ref[...]
    shift = 2 * DEPTH + SLOT

    def spread(packed, f):
        moved = pltpu.roll(packed, (DEPTH - SLOT - SLOT * (f % SLOTS)) % LANES, 1)
        return jnp.where(at_edge, moved, 0.0)

    copies = []
    for g in range(groups):
        low = high = sources[0][g]
        for low_mask, high_mask, source in zip(low_masks, high_masks, sources[1:]):
            low = jnp.where(low_mask, source[g], low)
            high = jnp.where(high_mask, source[g], high)
        low_0 = pltpu.roll(low, shift, 1)
        low_1 = pltpu.roll(low, shift - 1, 1)
        low_2 = pltpu.roll(low, shift - 2, 1)
        high_1 = pltpu.roll(high, 1, 1)
        high_2 = pltpu.roll(high, 2, 1)
        damp = (
            low_damp[0] * low_0 + low_damp[1] * low_1 + low_damp[2] * low_2
            + high_damp[0] * high + high_damp[1] * high_1 + high_damp[2] * high_2
        )
        if g * SLOTS < halves:
            lapl_ref[g] = (
                low_lapl[0] * low_1 + low_lapl[1] * low_2
                + high_lapl[0] * high_1 + high_lapl[1] * high_2
            )
        first = g * SLOTS
        last = min(first + SLOTS, fields)
        for f in range(first, last):
            rate = spread(damp, f)
            if f >= halves:
                rate = rate + half * spread(lapl_ref[(f - halves) // SLOTS], f - halves)
            next_buf[f] = next_ref[f] + (SECTION_SHIFT * TIME_STEP) * rate
            total_buf[f] = total_ref[f] + (SECTION_WEIGHT * TIME_STEP) * rate
        part = pl.ds(first, last - first)
        for which, (buf, out) in enumerate(((next_buf, next_out), (total_buf, total_out))):
            copy = pltpu.make_async_copy(buf.at[part], out.at[part], sems.at[which, g])
            copy.start()
            copies.append(copy)
    for copy in copies:
        copy.wait()


def swap_ends(ends, axis):
    count = lax.axis_size(axis)
    if count == 2:
        return lax.ppermute(ends, axis, [(0, 1), (1, 0)])
    low, high = jnp.split(ends, 2, axis=1)
    forward = [(i, (i + 1) % count) for i in range(count)]
    backward = [(target, source) for source, target in forward]
    return jnp.concatenate([lax.ppermute(low, axis, backward), lax.ppermute(high, axis, forward)], axis=1)


def routed(packed, owner):
    columns = lax.axis_size("gz")
    labels = jnp.arange(columns, dtype=jnp.int32)
    matches = owner[:, None] == labels[None, :]
    column_of = jnp.sum(jnp.where(matches, labels[:, None], 0), axis=0)
    below = jnp.take(owner, (column_of + columns - 1) % columns)
    above = jnp.take(owner, (column_of + 1) % columns)
    groups, rows, _ = packed.shape
    pieces = packed.reshape(groups, columns, rows // columns, LANES).transpose(1, 0, 2, 3)
    spread = lax.all_to_all(pieces, "gz", split_axis=0, concat_axis=0, tiled=True)
    low_part = (jnp.arange(LANES) % DEPTH) % SLOT < GHOST
    forwarded = jnp.where(low_part, spread[below], spread[above])
    arrived = lax.all_to_all(forwarded, "gz", split_axis=0, concat_axis=0, tiled=True)
    return arrived.transpose(1, 0, 2, 3).reshape(groups, rows, LANES)


def substep(state, base, accum, owner):
    fields, thickness, _, cells = state.shape
    per_layer = cells // LANES
    rows = thickness * per_layer
    shape = (fields, rows, LANES)
    columns = lax.axis_size("gz")
    me = lax.axis_index("gz").reshape(1).astype(jnp.int32)
    cells_in = state.reshape(shape)
    base = base.reshape(shape)
    accum = accum.reshape(shape)
    groups = -(-fields // SLOTS)
    f32 = lambda *s: jax.ShapeDtypeStruct(s, jnp.float32)
    whole = fields * rows * LANES * 4
    smem = pl.BlockSpec(memory_space=SMEM)
    anywhere = pl.BlockSpec(memory_space=pl.ANY)

    packed = call(pack_faces_kernel, f32(groups, rows, LANES), [vmem_spec()], cost=(whole, whole))(cells_in)
    if direct(columns):
        near = columns // 2
        cross = columns // 2 + columns // 4
        got = []
        for d in range(1, near):
            got.append(exchange(packed, d))
        forwarded = call(
            functools.partial(forward_kernel, columns, cross), f32(groups, rows, LANES),
            [smem, smem] + [vmem_spec() for _ in range(near)], cost=(whole, whole),
        )(owner, me, packed, *got)
        candidates = [exchange(forwarded, cross)] + got
    else:
        candidates = [routed(packed, owner)]

    layers, strips = call(
        functools.partial(pack_ends_kernel, per_layer),
        [f32(fields, 2 * GHOST * per_layer, LANES), f32(fields, 2 * thickness, LANES)],
        [vmem_spec()], cost=(whole, whole),
    )(cells_in)
    layers = swap_ends(layers, "gx")
    strips = swap_ends(strips, "gy")
    edge = GHOST * per_layer
    count = fields // 4
    reach = -(-edge // 8) * 8
    rolls = [VMEM((rows + 2 * edge, LANES), jnp.float32), VMEM((rows, LANES), jnp.float32), VMEM((rows, LANES), jnp.float32)]
    part_next, part_total, half, pull = call(
        functools.partial(early_kernel, per_layer, count),
        [f32(*shape), f32(*shape), f32(rows, LANES), f32(rows, LANES)],
        [vmem_spec() for _ in range(4)],
        scratch=rolls, cost=(30 * whole, 3 * whole),
    )(cells_in, strips, base, accum)
    part_next, part_total = call(
        functools.partial(late_kernel, per_layer, count),
        [f32(*shape), f32(*shape)],
        [vmem_spec() for _ in range(9)],
        scratch=rolls + [VMEM((edge + reach, LANES), jnp.float32), VMEM((edge + reach, LANES), jnp.float32)],
        cost=(30 * whole, 3 * whole), aliases={7: 0, 8: 1},
    )(cells_in, layers, strips, base, accum, half, pull, part_next, part_total)
    next_section, accum_out = call(
        functools.partial(final_kernel, columns), [f32(*shape), f32(*shape)],
        [smem, smem] + [vmem_spec() for _ in range(3 + len(candidates))],
        out_specs=[anywhere, anywhere],
        scratch=[VMEM((-(-(fields // 2) // SLOTS), rows, LANES), jnp.float32)]
        + [VMEM(shape, jnp.float32) for _ in range(2)]
        + [pltpu.SemaphoreType.DMA((2, groups))],
        cost=(10 * whole, 4 * whole),
    )(owner, me, half, part_next, part_total, *candidates)
    return (next_section.reshape(state.shape), accum_out.reshape(state.shape))


def direct(columns):
    return 2 < columns <= 8 and columns & (columns - 1) == 0


def exchange(x, d):
    columns = lax.axis_size("gz")
    return lax.ppermute(x, "gz", [(i, i ^ d) for i in range(columns)])


def solution(mesh):
    step = jax.shard_map(
        substep,
        mesh=mesh,
        in_specs=(
            P(None, "gx", ("gy", "gz"), None),
            P(None, "gx", ("gy", "gz"), None),
            P(None, "gx", ("gy", "gz"), None),
            P(),
        ),
        out_specs=(P(None, "gx", ("gy", "gz"), None), P(None, "gx", ("gy", "gz"), None)),
        check_vma=False,
    )
    columns = mesh.shape["gz"]
    if not direct(columns):
        return step
    return step
```

```python
import functools
import math

import jax
import jax.numpy as jnp
from jax import lax
from jax.experimental import pallas as pl
from jax.experimental.pallas import tpu as pltpu
from jax.sharding import PartitionSpec as P


BLOCK = 16


DAMPING_STRENGTH = 1.0
SPACING = 1.0
TIME_STEP = 0.25
SECTION_SHIFT = 0.5
SECTION_WEIGHT = 1.0 / 3.0

LANES = 128
TILE = 8
LIMIT = 16 * 2**20
GHOST = 3
SLOT = 2 * GHOST
DEPTH = 2 * BLOCK
ARRAYS = math.lcm(DEPTH, SLOT) // DEPTH
SLOTS = ARRAYS * DEPTH // SLOT
DAMP = DAMPING_STRENGTH / (64.0 * SPACING)
LAPL = 1.0 / (12.0 * SPACING * SPACING)
VMEM = pltpu.VMEM
SMEM = pltpu.SMEM


def vmem_spec():
    return pl.BlockSpec(memory_space=VMEM)


def call(kernel, outs, in_specs, out_specs=None, scratch=(), cost=None):
    multiple = isinstance(outs, (list, tuple))
    if out_specs is None:
        out_specs = [vmem_spec() for _ in outs] if multiple else vmem_spec()
    return pl.pallas_call(
        kernel,
        out_shape=outs,
        in_specs=in_specs,
        out_specs=out_specs,
        scratch_shapes=list(scratch),
        compiler_params=pltpu.CompilerParams(vmem_limit_bytes=LIMIT),
        cost_estimate=pl.CostEstimate(flops=cost[0], bytes_accessed=cost[1], transcendentals=0),
    )


def lane_index(rows):
    return lax.broadcasted_iota(jnp.int32, (rows, LANES), 1)


def blocks(fields):
    whole = fields - fields % SLOTS
    out = [[(first + k, half) for k in range(SLOTS)] for first in range(0, whole, SLOTS) for half in (0, 1)]
    rest = range(whole, fields)
    assert len(rest) in (0, SLOTS // 2)
    return out + ([[(f, half) for half in (0, 1) for f in rest]] if rest else [])


def half_rows(half, rows):
    return slice(half * rows, (half + 1) * rows)


def plane(array, lane):
    return array * DEPTH + lane % DEPTH


def pack_faces_kernel(state_ref, out_ref):
    rows = out_ref.shape[2]
    lane = lane_index(rows)
    for at, block in enumerate(blocks(state_ref.shape[0])):
        moved = [
            pltpu.roll(state_ref[f, half_rows(half, rows)], (GHOST + SLOT * k) % LANES, 1)
            for k, (f, half) in enumerate(block)
        ]
        for array in range(ARRAYS):
            slot = plane(array, lane) // SLOT
            first = array * DEPTH // SLOT
            packed = moved[first]
            for k in range(first + 1, (array * DEPTH + DEPTH - 1) // SLOT + 1):
                packed = jnp.where(slot == k, moved[k], packed)
            out_ref[at, array] = packed


def pack_ends_kernel(per_layer, state_ref, layers_ref, strips_ref):
    fields, rows, _ = state_ref.shape
    edge = GHOST * per_layer
    layers = rows // per_layer
    layers_ref[:, :edge] = state_ref[:, :edge]
    layers_ref[:, edge:] = state_ref[:, rows - edge :]
    for f in range(fields):
        strips_ref[f, :layers] = state_ref[f, pl.ds(0, layers, stride=per_layer)]
        strips_ref[f, layers:] = state_ref[f, pl.ds(per_layer - 1, layers, stride=per_layer)]


def find_column(owner_ref, device, columns):
    def body(t, found):
        return jnp.where(owner_ref[t] == device, t, found)

    return lax.fori_loop(0, columns, body, jnp.int32(0))


def neighbours(owner_ref, device, columns):
    column = find_column(owner_ref, device, columns)
    below = owner_ref[lax.rem(column + columns - 1, columns)]
    above = owner_ref[lax.rem(column + 1, columns)]
    return below, above


def routes_kernel(columns, cross, owner_ref, me_ref, out_ref):
    me = me_ref[0]
    below, above = neighbours(owner_ref, me, columns)
    there, beyond = neighbours(owner_ref, me ^ cross, columns)
    shape = out_ref.shape[1:]
    for array in range(ARRAYS):
        low_part = plane(array, lane_index(shape[0])) % SLOT < GHOST
        out_ref[array] = jnp.where(low_part, me ^ there, me ^ beyond)
    out_ref[ARRAYS] = jnp.full(shape, me ^ below, jnp.int32)
    out_ref[ARRAYS + 1] = jnp.full(shape, me ^ above, jnp.int32)


def tiles(rows):
    return [slice(start, start + TILE) for start in range(0, rows, TILE)]


def forward_kernel(routes_ref, *refs):
    *sources, out_ref = refs
    count, arrays, rows, _ = out_ref.shape
    for array in range(arrays):
        masks = [routes_ref[array] == d for d in range(1, len(sources))]
        for block in range(count):
            for at in tiles(rows):
                chosen = sources[0][block, array, at]
                for mask, source in zip(masks, sources[1:]):
                    chosen = jnp.where(mask, source[block, array, at], chosen)
                out_ref[block, array, at] = chosen


def field_sums(per_layer, lane, state_ref, strips_ref, f, wide_ref, after_ref, before_ref):
    rows = state_ref.shape[1]
    edge = GHOST * per_layer
    layers = rows // per_layer
    depth = lane % DEPTH
    here = state_ref[f]
    wide_ref[edge : edge + rows] = here
    after_ref[...] = wide_ref[edge + 1 : edge + 1 + rows]
    before_ref[...] = wide_ref[edge - 1 : edge - 1 + rows]
    after_ref[pl.ds(per_layer - 1, layers, stride=per_layer)] = strips_ref[f, :layers]
    before_ref[pl.ds(0, layers, stride=per_layer)] = strips_ref[f, layers:]
    after = after_ref[...]
    before = before_ref[...]
    sums = []
    for k in range(1, GHOST + 1):
        low = edge - k * per_layer
        high = edge + k * per_layer
        total = wide_ref[low : low + rows] + wide_ref[high : high + rows]
        step = DEPTH * k
        total += pltpu.roll(jnp.where(lane >= step, here, after), LANES - step, 1)
        total += pltpu.roll(jnp.where(lane < LANES - step, here, before), step, 1)
        total += pltpu.roll(jnp.where(depth >= k, here, 0.0), LANES - k, 1)
        total += pltpu.roll(jnp.where(depth < DEPTH - k, here, 0.0), k, 1)
        sums.append(total)
    return here, sums


def pair_rates(here, curvature, metric_sums, curvature_sums, half, pull):
    one, two, three = metric_sums
    damping = (three - 6.0 * two + 15.0 * one - 60.0 * here) * DAMP
    laplace = (16.0 * one - two - 90.0 * here) * LAPL
    metric_rate = 4.0 * half * curvature + damping
    one, two, three = curvature_sums
    damping = (three - 6.0 * two + 15.0 * one - 60.0 * curvature) * DAMP
    return metric_rate, half * laplace + pull * curvature + damping


def early_kernel(per_layer, count, state_ref, strips_ref, rates_ref, half_ref, pull_ref, wide_ref, after_ref, before_ref):
    fields, rows, _ = state_ref.shape
    halves = fields // 2
    edge = GHOST * per_layer
    lane = lane_index(rows)
    lapse = 1.0 + 0.25 * jnp.tanh(state_ref[0])
    trace = state_ref[halves]
    for f in range(halves + 1, fields):
        trace = trace + state_ref[f]
    half_ref[...] = -0.5 * lapse
    pull_ref[...] = lapse * trace * (1.0 / halves)
    wide_ref[:edge] = jnp.zeros((edge, LANES), jnp.float32)
    wide_ref[edge + rows :] = jnp.zeros((edge, LANES), jnp.float32)

    def body(f, carry):
        sums = lambda at: field_sums(per_layer, lane, state_ref, strips_ref, at, wide_ref, after_ref, before_ref)
        u, u_sums = sums(f)
        v, v_sums = sums(f + halves)
        rates_ref[f], rates_ref[f + count] = pair_rates(u, v, u_sums, v_sums, half_ref[...], pull_ref[...])
        return carry

    lax.fori_loop(0, count, body, 0)


def late_kernel(
    per_layer, count, state_ref, layers_ref, strips_ref, base_ref, accum_ref, half_ref, pull_ref, rates_ref,
    next_ref, total_ref, wide_ref, after_ref, before_ref, low_ref, high_ref,
):
    fields, rows, _ = state_ref.shape
    halves = fields // 2
    edge = GHOST * per_layer
    reach = -(-edge // TILE) * TILE
    lane = lane_index(rows)
    low_ref[edge:] = jnp.zeros((reach, LANES), jnp.float32)
    high_ref[:reach] = jnp.zeros((reach, LANES), jnp.float32)

    def write(f, at, rate):
        next_ref[f, at] = base_ref[f, at] + (SECTION_SHIFT * TIME_STEP) * rate
        total_ref[f, at] = accum_ref[f, at] + (SECTION_WEIGHT * TIME_STEP) * rate

    def ends(f):
        low_ref[:edge] = layers_ref[f, edge:]
        high_ref[reach:] = layers_ref[f, :edge]
        out = []
        for buf, at in ((low_ref, lambda k: edge - k * per_layer), (high_ref, lambda k: k * per_layer)):
            one, two, three = (buf[at(k) : at(k) + reach] for k in (1, 2, 3))
            out.append(((three - 6.0 * two + 15.0 * one) * DAMP, (16.0 * one - two) * LAPL))
        return out

    def mend(f, carry):
        for at, u, v in zip((slice(0, reach), slice(rows - reach, rows)), ends(f), ends(f + halves)):
            write(f, at, rates_ref[f, at] + u[0])
            write(f + halves, at, rates_ref[f + count, at] + v[0] + half_ref[at] * u[1])
        inner = slice(reach, rows - reach)
        write(f, inner, rates_ref[f, inner])
        write(f + halves, inner, rates_ref[f + count, inner])
        return carry

    lax.fori_loop(0, count, mend, 0)

    def body(f, carry):
        def sums(at):
            wide_ref[:edge] = layers_ref[at, edge:]
            wide_ref[edge + rows :] = layers_ref[at, :edge]
            return field_sums(per_layer, lane, state_ref, strips_ref, at, wide_ref, after_ref, before_ref)

        u, u_sums = sums(f)
        v, v_sums = sums(f + halves)
        rates = pair_rates(u, v, u_sums, v_sums, half_ref[...], pull_ref[...])
        write(f, slice(None), rates[0])
        write(f + halves, slice(None), rates[1])
        return carry

    lax.fori_loop(count, halves, body, 0)


def final_kernel(routes_ref, half_ref, next_ref, total_ref, *refs):
    count = len(refs) - 6
    sources = refs[:count]
    next_out, total_out, lapl_ref, next_buf, total_buf, sems = refs[count:]
    fields = next_ref.shape[0]
    halves = fields // 2
    rows = sources[0].shape[2]
    lane = lane_index(rows)
    depth = lane % DEPTH
    at_edge = (depth < GHOST) | (depth >= DEPTH - GHOST)
    low_masks, high_masks = (
        [jnp.concatenate([routes_ref[ARRAYS + side]] * (rows // TILE), axis=0) == d for d in range(1, count)]
        for side in (0, 1)
    )

    def chosen(block, array, masks):
        out = sources[0][block, array]
        for mask, source in zip(masks, sources[1:]):
            out = jnp.where(mask, source[block, array], out)
        return out

    def edge_rates(block):
        low = [chosen(block, array, low_masks) for array in range(ARRAYS)]
        high = [chosen(block, array, high_masks) for array in range(ARRAYS)]
        back = LANES - 2 * DEPTH + SLOT
        low = [[pltpu.roll(x, back - i, 1) for x in low] for i in range(GHOST)]
        high = [high] + [[pltpu.roll(x, i, 1) for x in high] for i in range(1, GHOST)]
        damping, laplace = [], []
        for array in range(ARRAYS):
            s = plane(array, lane) % SLOT
            is_low = s < GHOST
            near = [
                jnp.where(
                    is_low,
                    jnp.where(depth < SLOT - i, low[i][array - 1], low[i][array]),
                    jnp.where(depth < i, high[i][array - 1], high[i][array]) if i else high[0][array],
                )
                for i in range(GHOST)
            ]
            inner = (s == GHOST - 1) | (s == GHOST)
            outer = (s == 0) | (s == SLOT - 1)
            one = jnp.where(inner, 0.0, near[1])
            two = jnp.where(outer, near[2], 0.0)
            damping.append((near[0] - 6.0 * one + 15.0 * two) * DAMP)
            laplace.append((16.0 * two - one) * LAPL)
        return damping, laplace

    def spread(planes, k):
        first = (SLOT * k + GHOST) // DEPTH
        last = (SLOT * (k + 1) + GHOST - 1) // DEPTH % ARRAYS
        value = planes(first)
        if last != first:
            value = jnp.where(depth < DEPTH // 2, planes(last), value)
        return jnp.where(at_edge, pltpu.roll(value, (DEPTH - SLOT - SLOT * k) % LANES, 1), 0.0)

    layout = blocks(fields)
    place = {pair: (at, k) for at, block in enumerate(layout) for k, pair in enumerate(block)}
    copies = []
    for at, block in enumerate(layout):
        damping, laplace = edge_rates(at)
        if any(f < halves for f, _ in block):
            for array in range(ARRAYS):
                lapl_ref[at, array] = laplace[array]
        for part in range(2):
            piece = block[part * SLOTS // 2 : (part + 1) * SLOTS // 2]
            for k, (f, half) in enumerate(piece, part * SLOTS // 2):
                here = half_rows(half, rows)
                rate = spread(lambda array: damping[array], k)
                if f >= halves:
                    source, slot = place[(f - halves, half)]
                    rate = rate + half_ref[here] * spread(lambda array: lapl_ref[source, array], slot)
                next_buf[f, here] = next_ref[f, here] + (SECTION_SHIFT * TIME_STEP) * rate
                total_buf[f, here] = total_ref[f, here] + (SECTION_WEIGHT * TIME_STEP) * rate
            (first, half), (last, _) = piece[0], piece[-1]
            box = (pl.ds(first, last + 1 - first), pl.ds(half * rows, rows))
            for which, (buf, out) in enumerate(((next_buf, next_out), (total_buf, total_out))):
                copy = pltpu.make_async_copy(buf.at[box], out.at[box], sems.at[which, 2 * at + part])
                copy.start()
                copies.append(copy)
    for copy in copies:
        copy.wait()


def swap_ends(ends, axis):
    count = lax.axis_size(axis)
    if count == 2:
        return lax.ppermute(ends, axis, [(0, 1), (1, 0)])
    low, high = jnp.split(ends, 2, axis=1)
    forward = [(i, (i + 1) % count) for i in range(count)]
    backward = [(target, source) for source, target in forward]
    return jnp.concatenate([lax.ppermute(low, axis, backward), lax.ppermute(high, axis, forward)], axis=1)


def routed(packed, owner):
    columns = lax.axis_size("gz")
    labels = jnp.arange(columns, dtype=jnp.int32)
    matches = owner[:, None] == labels[None, :]
    column_of = jnp.sum(jnp.where(matches, labels[:, None], 0), axis=0)
    below = jnp.take(owner, (column_of + columns - 1) % columns)
    above = jnp.take(owner, (column_of + 1) % columns)
    total = math.prod(packed.shape[:-1])
    piece = -(-total // columns)
    pieces = lambda x: jnp.pad(x.reshape(total, LANES), ((0, piece * columns - total), (0, 0))).reshape(columns, piece, LANES)
    planes = jnp.arange(ARRAYS)[:, None] * DEPTH + jnp.arange(LANES) % DEPTH
    low_part = jnp.broadcast_to((planes % SLOT < GHOST)[None, :, None, :], packed.shape)
    low_part = pieces(low_part)[lax.axis_index("gz")]
    spread = lax.all_to_all(pieces(packed), "gz", split_axis=0, concat_axis=0, tiled=True)
    forwarded = jnp.where(low_part, spread[below], spread[above])
    arrived = lax.all_to_all(forwarded, "gz", split_axis=0, concat_axis=0, tiled=True)
    return arrived.reshape(piece * columns, LANES)[:total].reshape(packed.shape)


def substep(state, base, accum, owner):
    fields, thickness, _, cells = state.shape
    per_layer = cells // LANES
    rows = thickness * per_layer
    shape = (fields, rows, LANES)
    columns = lax.axis_size("gz")
    me = lax.axis_index("gz").reshape(1).astype(jnp.int32)
    cells_in = state.reshape(shape)
    base = base.reshape(shape)
    accum = accum.reshape(shape)
    faces = (len(blocks(fields)), ARRAYS, rows // 2, LANES)
    f32 = lambda *s: jax.ShapeDtypeStruct(s, jnp.float32)
    whole = fields * rows * LANES * 4
    smem = pl.BlockSpec(memory_space=SMEM)
    anywhere = pl.BlockSpec(memory_space=pl.ANY)

    packed = call(pack_faces_kernel, f32(*faces), [vmem_spec()], cost=(whole, whole))(cells_in)
    cross = columns // 2 + columns // 4 if direct(columns) else 0
    routes = call(
        functools.partial(routes_kernel, columns, cross),
        jax.ShapeDtypeStruct((ARRAYS + 2, TILE, LANES), jnp.int32), [smem, smem], cost=(whole // 4, whole // 4),
    )(owner, me)
    if direct(columns):
        near = columns // 2
        got = []
        for d in range(1, near):
            got.append(exchange(packed, d))
        forwarded = call(
            forward_kernel, f32(*faces),
            [vmem_spec() for _ in range(near + 1)], cost=(whole, whole),
        )(routes, packed, *got)
        candidates = [exchange(forwarded, cross)] + got
    else:
        candidates = [routed(packed, owner)]

    layers, strips = call(
        functools.partial(pack_ends_kernel, per_layer),
        [f32(fields, 2 * GHOST * per_layer, LANES), f32(fields, 2 * thickness, LANES)],
        [vmem_spec()], cost=(whole, whole),
    )(cells_in)
    layers = swap_ends(layers, "gx")
    strips = swap_ends(strips, "gy")
    edge = GHOST * per_layer
    count = fields // 4
    reach = -(-edge // TILE) * TILE
    rolls = [VMEM((rows + 2 * edge, LANES), jnp.float32), VMEM((rows, LANES), jnp.float32), VMEM((rows, LANES), jnp.float32)]
    rates, half, pull = call(
        functools.partial(early_kernel, per_layer, count),
        [f32(2 * count, rows, LANES), f32(rows, LANES), f32(rows, LANES)],
        [vmem_spec() for _ in range(2)], scratch=rolls, cost=(30 * whole, 3 * whole),
    )(cells_in, strips)
    part_next, part_total = call(
        functools.partial(late_kernel, per_layer, count), [f32(*shape), f32(*shape)],
        [vmem_spec() for _ in range(8)],
        scratch=rolls + [VMEM((edge + reach, LANES), jnp.float32), VMEM((edge + reach, LANES), jnp.float32)],
        cost=(30 * whole, 3 * whole),
    )(cells_in, layers, strips, base, accum, half, pull, rates)
    next_section, accum_out = call(
        final_kernel, [f32(*shape), f32(*shape)],
        [vmem_spec() for _ in range(4 + len(candidates))],
        out_specs=[anywhere, anywhere],
        scratch=[VMEM(faces, jnp.float32)]
        + [VMEM(shape, jnp.float32) for _ in range(2)]
        + [pltpu.SemaphoreType.DMA((2, 2 * faces[0]))],
        cost=(10 * whole, 4 * whole),
    )(routes, half, part_next, part_total, *candidates)
    return (next_section.reshape(state.shape), accum_out.reshape(state.shape))


def direct(columns):
    return 2 < columns <= 8 and columns & (columns - 1) == 0


def exchange(x, d):
    columns = lax.axis_size("gz")
    return lax.ppermute(x, "gz", [(i, i ^ d) for i in range(columns)])


def solution(mesh):
    step = jax.shard_map(
        substep,
        mesh=mesh,
        in_specs=(
            P(None, "gx", ("gy", "gz"), None),
            P(None, "gx", ("gy", "gz"), None),
            P(None, "gx", ("gy", "gz"), None),
            P(),
        ),
        out_specs=(P(None, "gx", ("gy", "gz"), None), P(None, "gx", ("gy", "gz"), None)),
        check_vma=False,
    )
    columns = mesh.shape["gz"]
    if not direct(columns):
        return step
    return step
```
